32 devices in a mesh: groups: 2 (over y), segment: 2 (over core), seq: 8 (over z, x).
Axes of the slice: x: 2, y: 2, z: 4, core: 2. Of those that a mesh axis runs over, the one named last changes fastest.
Arguments:
- held: bfloat16 [2, 32, 8, 16, 640], P('segment', ('groups', 'seq')), parts along dimension 1, may hold values from -6 to 6
- arrivals: bfloat16 [3, 32, 8, 16, 640], P(None, ('groups', 'seq')), parts along dimension 1, may hold values from -6 to 6
- spatial_weight: bfloat16 [2, 9, 640, 640], P('segment'), may hold values from -0.078125 to 0.078125
- spatial_scale: float32 [2, 5, 640], P('segment'), may hold values from 0.5 to 2
- temporal_weight: bfloat16 [2, 3, 640, 640], P('segment'), may hold values from -0.125 to 0.125
- temporal_scale: float32 [2, 5, 640], P('segment'), may hold values from 0.5 to 2
Outputs:
- emitted: bfloat16 [2, 4, 32, 8, 16, 640], P('segment', None, ('groups', 'seq')), parts along dimension 2
The draws below stay inside these ranges and needn't reach their ends.
There are 2 independent parts, one for each index of `groups`. The reference program is written for one: setup_inputs(seed, part) draws one part's arguments, and reference() takes and returns one part's arrays. A program takes and returns all parts, laid end to end along the dimension named above; an argument that names none is the same for every part. Nothing has to cross between parts.
All inputs are finite; a program needn't handle non-finite values.
Results may differ from the reference program's by a relative error of at most 0.014.
Values may be sent and summed in bfloat16 or wider, within the bound.
No kernel may reach another device: no remote copies, remote signals or barrier semaphores. Data moves between devices by JAX's collectives and lax.ppermute only.
A program may use at most 128 MiB of HBM per device.

```python
import math
import jax
import jax.numpy as jnp

C = 640
BLOCK = 128
H = 8
W = 16
TICKS = 4
SECTIONS = 2
FRAMES = 16
N_SEGMENT = 2


def block_levels(stream_key, dims, shards, least, top_value):
    level, own = 1.0, jax.random.fold_in(stream_key, 6)
    for dim, blocks in shards:
        steps = jnp.exp(jax.random.uniform(jax.random.fold_in(own, dim), (blocks,), jnp.float32, least / len(shards), top_value / len(shards)))
        level = level * jnp.repeat(steps, dims[dim] // blocks).reshape([-1 if axis == dim else 1 for axis in range(len(dims))])
    return level


def centred(key, extent, spread, reach, split=(), kind=jnp.bfloat16):
    array = spread * jax.random.normal(key, extent, jnp.float32)
    if split:
        array = array * block_levels(key, extent, split, -0.22, 0.18)
    return jnp.clip(array, -reach, reach).astype(kind)


def setup_inputs(seed: int = 0, part: int = 0) -> dict:
    key_list = jax.random.split(jax.random.key(seed), 7)
    own_keys = jax.random.split(jax.random.fold_in(key_list[6], part), 7)
    held = centred(own_keys[0], (N_SEGMENT, FRAMES, H, W, C), 1.0, 6.0, ((0, 2), (1, 8)))
    arrivals = centred(own_keys[1], (TICKS - 1, FRAMES, H, W, C), 1.0, 6.0, ((1, 8),))
    spatial_weight = centred(key_list[2], (SECTIONS, 9, C, C), (9 * C) ** -0.5, 0.078125, ((0, 2),))
    spatial_scale = jnp.clip(jnp.exp(math.log(2.0) - 1.3862944 * jax.random.uniform(key_list[3], (SECTIONS, C // BLOCK, C), jnp.float32) ** block_levels(key_list[3], (SECTIONS, C // BLOCK, C), ((0, 2),), -0.2, 0.2)), 0.5, 2.0)
    temporal_weight = centred(key_list[4], (SECTIONS, 3, C, C), (3 * C) ** -0.5, 0.125, ((0, 2),))
    temporal_scale = jnp.clip(jnp.exp(math.log(2.0) - 1.3862944 * jax.random.uniform(key_list[5], (SECTIONS, C // BLOCK, C), jnp.float32) ** block_levels(key_list[5], (SECTIONS, C // BLOCK, C), ((0, 2),), -0.2, 0.2)), 0.5, 2.0)
    return dict(held=held, arrivals=arrivals, spatial_weight=spatial_weight, spatial_scale=spatial_scale, temporal_weight=temporal_weight, temporal_scale=temporal_scale)


def dequantize(weights, scales):
    block = weights.shape[1] // scales.shape[0]
    expanded = jnp.repeat(scales, block, axis=0)
    return (weights.astype(jnp.float32) * expanded[None]).astype(jnp.bfloat16)


def spatial_term(activation, kernels):
    frames, height, width, channels = activation.shape
    padded = jnp.pad(activation, ((0, 0), (1, 1), (1, 1), (0, 0)))
    total = jnp.zeros((frames * height * width, channels), jnp.float32)
    for row_tap in range(3):
        for col_tap in range(3):
            window = padded[:, row_tap:row_tap + height, col_tap:col_tap + width].reshape(-1, channels)
            total = total + jnp.dot(window, kernels[row_tap * 3 + col_tap], preferred_element_type=jnp.float32)
    return total.reshape(activation.shape)


def temporal_term(activation, kernels):
    frames = activation.shape[0]
    channels = activation.shape[-1]
    blank = jnp.zeros((1,) + activation.shape[1:], activation.dtype)
    padded = jnp.concatenate([blank, activation, blank], axis=0)
    total = jnp.zeros((activation.size // channels, channels), jnp.float32)
    for frame_tap in range(3):
        window = padded[frame_tap:frame_tap + frames].reshape(-1, channels)
        total = total + jnp.dot(window, kernels[frame_tap], preferred_element_type=jnp.float32)
    return total.reshape(activation.shape).astype(jnp.bfloat16)


def section(activation, spatial_kernels, temporal_kernels):
    lifted = jax.nn.silu(activation.astype(jnp.float32)).astype(jnp.bfloat16)
    middle = (activation.astype(jnp.float32) + spatial_term(lifted, spatial_kernels)).astype(jnp.bfloat16)
    lifted_mid = jax.nn.silu(middle.astype(jnp.float32)).astype(jnp.bfloat16)
    temporal = temporal_term(lifted_mid, temporal_kernels)
    return (middle.astype(jnp.float32) + temporal.astype(jnp.float32)).astype(jnp.bfloat16)


def reference(held, arrivals, spatial_weight, spatial_scale, temporal_weight, temporal_scale):
    segments = held.shape[0]
    per_segment = spatial_weight.shape[0] // segments
    ticks = arrivals.shape[0] + 1
    spatial_kernels = [dequantize(spatial_weight[k], spatial_scale[k]) for k in range(spatial_weight.shape[0])]
    temporal_kernels = [dequantize(temporal_weight[k], temporal_scale[k]) for k in range(temporal_weight.shape[0])]
    inputs = [held[segment_index] for segment_index in range(segments)]
    collected = [[] for segment_index in range(segments)]
    for tick_index in range(ticks):
        outputs = []
        for segment_index in range(segments):
            current = inputs[segment_index]
            for inner in range(per_segment):
                number = segment_index * per_segment + inner
                current = section(current, spatial_kernels[number], temporal_kernels[number])
            outputs.append(current)
            collected[segment_index].append(current)
        if tick_index + 1 < ticks:
            inputs = [arrivals[tick_index]] + outputs[:-1]
    return jnp.stack([jnp.stack(series) for series in collected])
```

```python
import functools

import jax
import jax.numpy as jnp
from jax import lax
from jax.experimental import pallas as pl
from jax.experimental.pallas import tpu as pltpu
from jax.sharding import PartitionSpec as P

AXES = ("groups", "segment", "seq")
VMEM = pl.BlockSpec(memory_space=pltpu.VMEM)
ANY = pl.BlockSpec(memory_space=pl.ANY)


def silu(v):
    return v / (1.0 + jnp.exp(-v))


def swap_pairs(sizes, odd, active):
    groups, segments, count = sizes

    def paired(segment, place):
        mate = place - 1 if (place + odd) % 2 else place + 1
        return mate if segment in active and 0 <= mate < count else None

    pairs = []
    for group in range(groups):
        for segment in range(segments):
            for place in range(count):
                mate = paired(segment, place)
                target = (group, segment, mate)
                if mate is None:
                    other = segment ^ 1
                    if other < segments and paired(other, place) is None:
                        target = (group, other, place)
                    elif group ^ 1 < groups:
                        target = (group ^ 1, segment, place)
                    else:
                        continue
                flat = lambda g, s, p: (g * segments + s) * count + p
                pairs.append((flat(group, segment, place), flat(*target)))
    return pairs


def spatial_kernel(slot, *refs):
    if slot == 0:
        x_ref, w_ref, s_ref = refs[:3]
        rest = refs[3:]
    else:
        first_ref, moved_ref, w_ref, s_ref = refs[:4]
        rest = refs[4:]
    mid_ref, lift_ref, even_ref, odd_ref, cols_ref = rest
    frames, height, width, channels = mid_ref.shape
    rows = frames * height * width
    blocks = s_ref.shape[0]
    block = channels // blocks
    segment = lax.axis_index("segment")
    place = lax.axis_index("seq")
    acc = jnp.zeros((rows, channels), jnp.float32)
    taps = w_ref.shape[0]
    inputs = []
    for b in range(blocks):
        part = pl.ds(b * block, block)
        if slot == 0:
            x = x_ref[:, :, :, part]
        else:
            x = jnp.where(segment == 0, first_ref[:, :, :, part], moved_ref[:, :, :, part])
        inputs.append(x)
        lifted = silu(x.astype(jnp.float32))
        edge = jnp.zeros((frames, height, 1, block), jnp.float32)
        line = jnp.zeros((frames, 1, width, block), jnp.bfloat16)
        for col in range(3):
            if col == 0:
                moved = jnp.concatenate([edge, lifted[:, :, :-1]], axis=2)
            elif col == 2:
                moved = jnp.concatenate([lifted[:, :, 1:], edge], axis=2)
            else:
                moved = lifted
            moved = moved.astype(jnp.bfloat16)
            for row in range(3):
                if row == 0:
                    window = jnp.concatenate([line, moved[:, :-1]], axis=1)
                elif row == 2:
                    window = jnp.concatenate([moved[:, 1:], line], axis=1)
                else:
                    window = moved
                cols_ref[b, :, pl.ds((row * 3 + col) * block, block)] = window.reshape(rows, block)
        weights = jnp.concatenate([w_ref[t, part, :] for t in range(taps)], axis=0)
        acc += jnp.dot(cols_ref[b], weights, preferred_element_type=jnp.float32) * s_ref[b : b + 1]
    x = jnp.concatenate(inputs, axis=3).reshape(rows, channels)
    mid = (x.astype(jnp.float32) + acc).astype(jnp.bfloat16)
    lift = silu(mid.astype(jnp.float32)).astype(jnp.bfloat16).reshape(mid_ref.shape)
    mid_ref[...] = mid.reshape(mid_ref.shape)
    lift_ref[...] = lift
    is_odd = lax.rem(place, 2) == 1
    even_ref[...] = jnp.where(is_odd, lift[0], lift[frames - 1])
    odd_ref[...] = jnp.where(is_odd, lift[frames - 1], lift[0])


def dequant_kernel(w_ref, s_ref, o_ref):
    blocks = s_ref.shape[0]
    block = w_ref.shape[1] // blocks
    for t in range(w_ref.shape[0]):
        for b in range(blocks):
            part = pl.ds(b * block, block)
            o_ref[t, part, :] = (w_ref[t, part, :].astype(jnp.float32) * s_ref[b : b + 1]).astype(
                jnp.bfloat16
            )


def temporal_kernel(slot, ticks, *refs):
    mid_ref, lift_ref, even_ref, odd_ref, w_ref = refs[:5]
    out_ref, res_ref, ext_ref, sem = refs[-4:]
    frames, height, width, channels = mid_ref.shape
    rows = frames * height * width
    segment = lax.axis_index("segment")
    place = lax.axis_index("seq")
    last = lax.axis_size("seq") - 1
    is_odd = lax.rem(place, 2) == 1
    zero = jnp.zeros((height, width, channels), jnp.bfloat16)
    even, odd = even_ref[...], odd_ref[...]
    left = jnp.where(is_odd, even, odd)
    right = jnp.where(is_odd, odd, even)
    ext_ref[0] = jnp.where(place == 0, zero, left)
    ext_ref[pl.ds(1, frames)] = lift_ref[...]
    ext_ref[frames + 1] = jnp.where(place == last, zero, right)
    acc = jnp.zeros((rows, channels), jnp.float32)
    for tap in range(w_ref.shape[0]):
        window = ext_ref[pl.ds(tap, frames)].reshape(rows, channels)
        acc += jnp.dot(window, w_ref[tap], preferred_element_type=jnp.float32)
    mid = mid_ref[...].reshape(rows, channels).astype(jnp.float32)
    res = (mid + acc.astype(jnp.bfloat16).astype(jnp.float32)).astype(jnp.bfloat16)
    res_ref[...] = res.reshape(res_ref.shape)
    tick = slot - segment
    valid = jnp.logical_and(tick >= 0, tick < ticks)

    @pl.when(valid)
    def _():
        copy = pltpu.make_async_copy(res_ref, out_ref.at[0, tick], sem)
        copy.start()
        copy.wait()


def params():
    return pltpu.CompilerParams(vmem_limit_bytes=24 << 20)


def spatial(slot, inputs, weights, scales):
    shape = inputs[0].shape
    frames, height, width, channels = shape
    rows = frames * height * width
    taps = weights.shape[0]
    blocks = scales.shape[0]
    clip = jax.ShapeDtypeStruct(shape, jnp.bfloat16)
    frame = jax.ShapeDtypeStruct(shape[1:], jnp.bfloat16)
    return pl.pallas_call(
        functools.partial(spatial_kernel, slot),
        out_shape=(clip, clip, frame, frame),
        in_specs=[VMEM] * (len(inputs) + 2),
        out_specs=[VMEM] * 4,
        scratch_shapes=[pltpu.VMEM((blocks, rows, taps * channels // blocks), jnp.bfloat16)],
        compiler_params=params(),
        cost_estimate=pl.CostEstimate(
            flops=2 * taps * rows * channels * channels,
            bytes_accessed=2 * taps * channels * channels,
            transcendentals=2 * rows * channels,
        ),
        name=f"spatial{slot}",
    )(*inputs, weights, scales)


def temporal(slot, ticks, mid, lift, even, odd, weights, out):
    shape = mid.shape
    frames, height, width, channels = shape
    rows = frames * height * width
    taps = weights.shape[0]
    operands = [mid, lift, even, odd, weights]
    aliases = {}
    if out is not None:
        aliases = {len(operands): 0}
        operands.append(out)
    return pl.pallas_call(
        functools.partial(temporal_kernel, slot, ticks),
        out_shape=(
            jax.ShapeDtypeStruct((1, ticks) + shape, jnp.bfloat16),
            jax.ShapeDtypeStruct(shape, jnp.bfloat16),
        ),
        in_specs=[VMEM] * 5 + [ANY] * len(aliases),
        out_specs=(ANY, VMEM),
        scratch_shapes=[
            pltpu.VMEM((frames + 2,) + shape[1:], jnp.bfloat16),
            pltpu.SemaphoreType.DMA,
        ],
        input_output_aliases=aliases,
        compiler_params=params(),
        cost_estimate=pl.CostEstimate(
            flops=2 * taps * rows * channels * channels,
            bytes_accessed=2 * taps * channels * channels,
            transcendentals=0,
        ),
        name=f"temporal{slot}",
    )(*operands)


def local(sizes, held, arrivals, spatial_weight, spatial_scale, temporal_weight, temporal_scale):
    groups, segments, count = sizes
    ticks = arrivals.shape[0] + 1
    slots = ticks + segments - 1
    held, weights_s, scales_s = held[0], spatial_weight[0], spatial_scale[0]
    weights_t = pl.pallas_call(
        dequant_kernel,
        out_shape=jax.ShapeDtypeStruct(temporal_weight.shape[1:], jnp.bfloat16),
        in_specs=[VMEM] * 2,
        out_specs=VMEM,
        compiler_params=params(),
        name="dequant",
    )(temporal_weight[0], temporal_scale[0])
    first = lax.axis_index("segment") == 0
    onward = [(s, (s + 1) % segments) for s in range(segments)]
    parts, results, out = [], [], None

    def finish(slot):
        nonlocal out
        mid, lift, even, odd = parts[slot]
        out, result = temporal(slot, ticks, mid, lift, even, odd, weights_t, out)
        results.append(result)

    for slot in range(slots):
        if slot == 0:
            inputs = [held]
        elif slot == 1:
            inputs = [arrivals[0], held]
        else:
            moved = lax.ppermute(results[slot - 2], "segment", onward)
            if slot - 1 < ticks - 1:
                inputs = [arrivals[slot - 1], moved]
            else:
                inputs = [moved, moved]
        mid, lift, even, odd = spatial(slot, inputs, weights_s, scales_s)
        active = [s for s in range(segments) if 0 <= slot - s < ticks]
        even = lax.ppermute(even, AXES, swap_pairs(sizes, 0, active))
        odd = lax.ppermute(odd, AXES, swap_pairs(sizes, 1, active))
        parts.append((mid, lift, even, odd))
        if slot >= 1:
            finish(slot - 1)
    finish(slots - 1)
    return out


def solution(mesh):
    sizes = tuple(mesh.shape[axis] for axis in AXES)
    in_specs = (
        P("segment", ("groups", "seq"), None, None, None),
        P(None, ("groups", "seq"), None, None, None),
        P("segment", None, None, None),
        P("segment", None, None),
        P("segment", None, None, None),
        P("segment", None, None),
    )
    out_specs = P("segment", None, ("groups", "seq"), None, None, None)
    return jax.shard_map(
        functools.partial(local, sizes),
        mesh=mesh,
        in_specs=in_specs,
        out_specs=out_specs,
        check_vma=False,
    )
```

```python
import functools

import jax
import jax.numpy as jnp
from jax import lax
from jax.experimental import pallas as pl
from jax.experimental.pallas import tpu as pltpu
from jax.sharding import PartitionSpec as P

AXES = ("groups", "segment", "seq")
VMEM = pl.BlockSpec(memory_space=pltpu.VMEM)
ANY = pl.BlockSpec(memory_space=pl.ANY)
HBM = pl.BlockSpec(memory_space=pltpu.HBM)


def silu(v):
    return v / (1.0 + jnp.exp(-v))


def swap_pairs(sizes, odd, active):
    groups, segments, count = sizes

    def paired(segment, place):
        mate = place - 1 if (place + odd) % 2 else place + 1
        return mate if segment in active and 0 <= mate < count else None

    pairs = []
    for group in range(groups):
        for segment in range(segments):
            for place in range(count):
                mate = paired(segment, place)
                target = (group, segment, mate)
                if mate is None:
                    other = segment ^ 1
                    if other < segments and paired(other, place) is None:
                        target = (group, other, place)
                    elif group ^ 1 < groups:
                        target = (group ^ 1, segment, place)
                    else:
                        continue
                flat = lambda g, s, p: (g * segments + s) * count + p
                pairs.append((flat(group, segment, place), flat(*target)))
    return pairs


def spatial_kernel(slot, *refs):
    if slot == 0:
        x_ref, hbm_ref, s_ref, mid_ref, lift_ref, even_ref, odd_ref, w_ref, cols_ref, sems = refs
    else:
        first_ref, moved_ref, w_ref, s_ref, mid_ref, lift_ref, even_ref, odd_ref, cols_ref = refs
    frames, height, width, channels = mid_ref.shape
    rows = frames * height * width
    blocks = cols_ref.shape[0]
    block = channels // blocks
    taps = w_ref.shape[0]
    copies = []
    if slot == 0:
        for b in range(blocks):
            part = pl.ds(b * block, block)
            copies.append(
                pltpu.make_async_copy(hbm_ref.at[:, part], w_ref.at[:, part], sems.at[b])
            )
            copies[-1].start()
    segment = lax.axis_index("segment")
    place = lax.axis_index("seq")
    tick = slot - 1
    acc = jnp.zeros((rows, channels), jnp.float32)
    inputs = []
    for b in range(blocks):
        part = pl.ds(b * block, block)
        if slot == 0:
            x = x_ref[:, :, :, part]
        elif tick >= first_ref.shape[0]:
            x = moved_ref[:, :, :, part]
        else:
            x = jnp.where(segment == 0, first_ref[tick, :, :, :, part], moved_ref[:, :, :, part])
        inputs.append(x)
        lifted = silu(x.astype(jnp.float32))
        edge = jnp.zeros((frames, height, 1, block), jnp.float32)
        line = jnp.zeros((frames, 1, width, block), jnp.bfloat16)
        for col in range(3):
            if col == 0:
                moved = jnp.concatenate([edge, lifted[:, :, :-1]], axis=2)
            elif col == 2:
                moved = jnp.concatenate([lifted[:, :, 1:], edge], axis=2)
            else:
                moved = lifted
            moved = moved.astype(jnp.bfloat16)
            for row in range(3):
                if row == 0:
                    window = jnp.concatenate([line, moved[:, :-1]], axis=1)
                elif row == 2:
                    window = jnp.concatenate([moved[:, 1:], line], axis=1)
                else:
                    window = moved
                cols_ref[b, :, pl.ds((row * 3 + col) * block, block)] = window.reshape(rows, block)
        if copies:
            copies[b].wait()
        weights = jnp.concatenate([w_ref[t, part, :] for t in range(taps)], axis=0)
        acc += jnp.dot(cols_ref[b], weights, preferred_element_type=jnp.float32) * s_ref[b]
    x = jnp.concatenate(inputs, axis=3).reshape(rows, channels)
    mid = (x.astype(jnp.float32) + acc).astype(jnp.bfloat16)
    lift = silu(mid.astype(jnp.float32)).astype(jnp.bfloat16).reshape(mid_ref.shape)
    mid_ref[...] = mid.reshape(mid_ref.shape)
    lift_ref[...] = lift
    is_odd = lax.rem(place, 2) == 1
    even_ref[...] = jnp.where(is_odd, lift[0], lift[frames - 1])
    odd_ref[...] = jnp.where(is_odd, lift[frames - 1], lift[0])


def dequant_kernel(w_ref, s_ref, o_ref):
    blocks = s_ref.shape[0]
    block = w_ref.shape[1] // blocks
    for b in range(blocks):
        part = pl.ds(b * block, block)
        for t in range(w_ref.shape[0]):
            o_ref[t, part, :] = (w_ref[t, part, :].astype(jnp.float32) * s_ref[b]).astype(
                jnp.bfloat16
            )


def temporal_kernel(slot, slots, ticks, *refs):
    mid_ref, lift_ref, even_ref, odd_ref, w_ref = refs[:5]
    out_ref, res_ref, ext_ref, sems = refs[-4:]
    frames, height, width, channels = mid_ref.shape
    rows = frames * height * width
    segment = lax.axis_index("segment")
    place = lax.axis_index("seq")
    last = lax.axis_size("seq") - 1
    is_odd = lax.rem(place, 2) == 1

    def emit(source, number, act):
        tick = number - segment

        @pl.when(jnp.logical_and(tick >= 0, tick < ticks))
        def _():
            act(pltpu.make_async_copy(source, out_ref.at[0, tick], sems.at[number % 2]))

    if slot > 0:
        before_ref = refs[5]
        emit(before_ref, slot - 1, lambda copy: copy.start())
    zero = jnp.zeros((height, width, channels), jnp.bfloat16)
    even, odd = even_ref[...], odd_ref[...]
    left = jnp.where(is_odd, even, odd)
    right = jnp.where(is_odd, odd, even)
    ext_ref[0] = jnp.where(place == 0, zero, left)
    ext_ref[pl.ds(1, frames)] = lift_ref[...]
    ext_ref[frames + 1] = jnp.where(place == last, zero, right)
    acc = jnp.zeros((rows, channels), jnp.float32)
    for tap in range(w_ref.shape[0]):
        window = ext_ref[pl.ds(tap, frames)].reshape(rows, channels)
        acc += jnp.dot(window, w_ref[tap], preferred_element_type=jnp.float32)
    mid = mid_ref[...].reshape(rows, channels).astype(jnp.float32)
    res = (mid + acc.astype(jnp.bfloat16).astype(jnp.float32)).astype(jnp.bfloat16)
    res_ref[...] = res.reshape(res_ref.shape)
    if slot == slots - 1:
        emit(res_ref, slot, lambda copy: copy.start())
        emit(res_ref, slot, lambda copy: copy.wait())
    if slot > 0:
        emit(before_ref, slot - 1, lambda copy: copy.wait())


def params(mebibytes=24):
    return pltpu.CompilerParams(vmem_limit_bytes=mebibytes << 20)


def spatial(slot, inputs, weights, scales):
    shape = inputs[-1].shape
    frames, height, width, channels = shape
    rows = frames * height * width
    taps = weights.shape[0]
    blocks = scales.shape[0]
    block = channels // blocks
    clip = jax.ShapeDtypeStruct(shape, jnp.bfloat16)
    frame = jax.ShapeDtypeStruct(shape[1:], jnp.bfloat16)
    out_shape = [clip, clip, frame, frame]
    scratch = [pltpu.VMEM((blocks, rows, taps * block), jnp.bfloat16)]
    weight_spec = VMEM
    if slot == 0:
        out_shape.append(jax.ShapeDtypeStruct(weights.shape, weights.dtype))
        scratch.append(pltpu.SemaphoreType.DMA((blocks,)))
        weight_spec = HBM
    return pl.pallas_call(
        functools.partial(spatial_kernel, slot),
        out_shape=out_shape,
        in_specs=[VMEM] * len(inputs) + [weight_spec, VMEM],
        out_specs=[VMEM] * len(out_shape),
        scratch_shapes=scratch,
        compiler_params=params(44 if slot == 0 else 24),
        cost_estimate=pl.CostEstimate(
            flops=2 * taps * rows * channels * channels,
            bytes_accessed=2 * taps * channels * channels,
            transcendentals=2 * rows * channels,
        ),
        name=f"spatial{slot}",
    )(*inputs, weights, scales)


def temporal(slot, slots, ticks, mid, lift, even, odd, weights, before, out):
    shape = mid.shape
    frames, height, width, channels = shape
    rows = frames * height * width
    taps = weights.shape[0]
    operands = [mid, lift, even, odd, weights]
    specs = [VMEM] * 5
    aliases = {}
    if slot > 0:
        operands.append(before)
        specs.append(VMEM)
    if slot > 1:
        aliases = {len(operands): 0}
        operands.append(out)
        specs.append(ANY)
    return pl.pallas_call(
        functools.partial(temporal_kernel, slot, slots, ticks),
        out_shape=(
            jax.ShapeDtypeStruct((1, ticks) + shape, jnp.bfloat16),
            jax.ShapeDtypeStruct(shape, jnp.bfloat16),
        ),
        in_specs=specs,
        out_specs=(ANY, VMEM),
        scratch_shapes=[
            pltpu.VMEM((frames + 2,) + shape[1:], jnp.bfloat16),
            pltpu.SemaphoreType.DMA((2,)),
        ],
        input_output_aliases=aliases,
        compiler_params=params(),
        cost_estimate=pl.CostEstimate(
            flops=2 * taps * rows * channels * channels,
            bytes_accessed=2 * taps * channels * channels,
            transcendentals=0,
        ),
        name=f"temporal{slot}",
    )(*operands)


def local(sizes, held, arrivals, spatial_weight, spatial_scale, temporal_weight, temporal_scale):
    groups, segments, count = sizes
    ticks = arrivals.shape[0] + 1
    slots = ticks + segments - 1
    held, weights_s = held[0], spatial_weight[0]
    scales_s = jnp.swapaxes(spatial_scale, 0, 1)
    weights_t = pl.pallas_call(
        dequant_kernel,
        out_shape=jax.ShapeDtypeStruct(temporal_weight.shape[1:], jnp.bfloat16),
        in_specs=[VMEM] * 2,
        out_specs=VMEM,
        compiler_params=params(),
        name="dequant",
    )(temporal_weight[0], jnp.swapaxes(temporal_scale, 0, 1))
    onward = [(s, (s + 1) % segments) for s in range(segments)]
    parts, results, out = [], [], None

    def finish(slot, after=None):
        nonlocal out
        mid, lift, even, odd = parts[slot]
        if after is not None:
            mid, _ = lax.optimization_barrier((mid, after))
        before = results[-1] if results else None
        out, result = temporal(slot, slots, ticks, mid, lift, even, odd, weights_t, before, out)
        results.append(result)

    for slot in range(slots):
        if slot == 0:
            inputs = [held]
        elif slot == 1:
            inputs = [arrivals, held]
        else:
            moved = lax.ppermute(results[slot - 2], "segment", onward)
            inputs = [arrivals, moved]
        made = spatial(slot, inputs, weights_s, scales_s)
        mid, lift, even, odd = made[:4]
        if slot == 0:
            weights_s = made[4]
        active = [s for s in range(segments) if 0 <= slot - s < ticks]
        even_in = lax.ppermute(even, AXES, swap_pairs(sizes, 0, active))
        odd_in = lax.ppermute(odd, AXES, swap_pairs(sizes, 1, active))
        parts.append((mid, lift, even_in, odd_in))
        if slot >= 1:
            finish(slot - 1, even)
    finish(slots - 1)
    return out


def solution(mesh):
    sizes = tuple(mesh.shape[axis] for axis in AXES)
    in_specs = (
        P("segment", ("groups", "seq"), None, None, None),
        P(None, ("groups", "seq"), None, None, None),
        P("segment", None, None, None),
        P("segment", None, None),
        P("segment", None, None, None),
        P("segment", None, None),
    )
    out_specs = P("segment", None, ("groups", "seq"), None, None, None)
    return jax.shard_map(
        functools.partial(local, sizes),
        mesh=mesh,
        in_specs=in_specs,
        out_specs=out_specs,
        check_vma=False,
    )
```
